32 devices in a mesh: groups: 2 (over y), enrol: 4 (over z), probe: 4 (over x, core).
Axes of the slice: x: 2, y: 2, z: 4, core: 2. Of those that a mesh axis runs over, the one named last changes fastest.
Arguments:
- images: float32 [16384, 512], P(('groups', 'enrol', 'probe')), parts along dimension 0, may hold values from -6 to 6
- w_first: float32 [512, 2048], replicated, may hold values from -0.25 to 0.25
- w_second: float32 [2048, 256], replicated, may hold values from -0.125 to 0.125
- calib_scale: float32 [1], replicated, may hold values from 5 to 20
- calib_bias: float32 [1], replicated, may hold values from -2 to 2
- template_slot: int32 [16384], P(('groups', 'enrol', 'probe')), parts along dimension 0, may hold values from 0 to 191
- media_counts: int32 [32, 16], P(('groups', 'enrol', 'probe')), parts along dimension 0, may hold values from 1 to 64, as said below
Outputs:
- scores: bfloat16 [4096, 1024], P(('groups', 'enrol'), 'probe'), parts along dimension 0
The draws below stay inside these ranges and needn't reach their ends.
There are 2 independent parts, one for each index of `groups`. The reference program is written for one: setup_inputs(seed, part) draws one part's arguments, and reference() takes and returns one part's arrays. A program takes and returns all parts, laid end to end along the dimension named above; an argument that names none is the same for every part. Nothing has to cross between parts.
Inputs may be any that keep to these rules, and one draw needn't show every extreme that they name: `media_counts`: each row sums to 512; in every draw one owner receives exactly 64 images from every device.
All inputs are finite; a program needn't handle non-finite values.
Results may differ from the reference program's by a relative error of at most 0.001.
Values sent between devices are 32-bit elements; how exact they have to be, the bound alone decides.
No kernel may reach another device: no remote copies, remote signals or barrier semaphores. Data moves between devices by JAX's collectives and lax.ppermute only.
A program may use at most 64 MiB of HBM per device.

```python
import math
import jax
import jax.numpy as jnp
from jax import lax

D_IN = 512
HIDDEN_SIZE = 2048
D_EMB = 256
IMG_DEV = 512
ET_OWN = 128
PT_OWN = 64
SLOTS = 192
IMAGES = 8192
ENROL = 2048
PROBE = 1024
N_ENROL = 4
N_PROBE = 4


def draw_media_counts(key, part):
    owners = N_ENROL * N_PROBE
    capacity = 2 * IMG_DEV // owners
    others = owners - 1
    per_owner = capacity - 1
    tickets = others * per_owner
    extra = IMG_DEV - capacity - others
    hot_owner = jax.random.randint(jax.random.fold_in(key, 7), (), 0, owners)
    owner_ids = jnp.arange(owners, dtype=jnp.int32)
    other_ids = jnp.arange(others, dtype=jnp.int32)
    rest_index = owner_ids - (owner_ids > hot_owner).astype(jnp.int32)
    rest_index = jnp.clip(rest_index, 0, others - 1)

    def one_row(row):
        row_key = jax.random.fold_in(jax.random.fold_in(key, 11), row)
        shuffled = jax.random.permutation(row_key, tickets).astype(jnp.int32)
        taken = jnp.arange(tickets, dtype=jnp.int32) < extra
        holder = shuffled // per_owner
        hits = (holder[:, None] == other_ids[None, :]) & taken[:, None]
        rest_counts = 1 + jnp.sum(hits.astype(jnp.int32), axis=0)
        counts = jnp.where(owner_ids == hot_owner, capacity, rest_counts[rest_index])
        return counts.astype(jnp.int32)
    return jax.vmap(one_row)(jnp.arange(owners, dtype=jnp.int32))


def plant(array, stream_key, least, largest):
    longest = array.shape.index(max(array.shape))
    spots = []
    for shift in (0, 1):
        where = [jax.random.randint(jax.random.fold_in(stream_key, axis), (), 0, length) for axis, length in enumerate(array.shape)]
        where[longest] = (where[longest] + shift) % array.shape[longest]
        spots.append(tuple(where))
    return array.at[spots[0]].set(least).at[spots[1]].set(largest)


def block_scale(stream_key, dims, pieces, low, largest):
    def one(dim, shards_of):
        heights = jax.random.uniform(jax.random.fold_in(jax.random.fold_in(stream_key, 6), dim), (shards_of,), jnp.float32, low / len(pieces), largest / len(pieces))
        return jnp.repeat(jnp.exp(heights), dims[dim] // shards_of).reshape((-1,) + (1,) * (len(dims) - dim - 1))

    gain = one(*pieces[0])
    for cut in pieces[1:]:
        gain = gain * one(*cut)
    return gain


def bell_draw(rng, dims, scale, bound, split=(), kind=jnp.bfloat16):
    loudness = block_scale(rng, dims, split, -0.22, 0.18) if split else 1.0
    array = jax.random.normal(rng, dims, jnp.float32) * scale * loudness
    return jnp.minimum(jnp.maximum(array, -bound), bound).astype(kind)


def setup_inputs(seed: int = 0, part: int = 0) -> dict:
    arg_keys = jax.random.split(jax.random.key(seed), 8)
    part_splits = jax.random.split(jax.random.fold_in(arg_keys[7], part), 8)
    images = bell_draw(part_splits[0], (IMAGES, D_IN), 1.0, 6.0, ((0, 16),), jnp.float32)
    w_first = bell_draw(arg_keys[1], (D_IN, HIDDEN_SIZE), D_IN ** -0.5, 0.25, (), jnp.float32)
    w_second = bell_draw(arg_keys[2], (HIDDEN_SIZE, D_EMB), HIDDEN_SIZE ** -0.5, 0.125, (), jnp.float32)
    calib_scale = jnp.clip(jnp.exp(jax.random.uniform(arg_keys[3], (1,), jnp.float32, math.log(5.0), math.log(20.0))), 5.0, 20.0)
    calib_bias = jnp.clip(jax.random.uniform(arg_keys[4], (1,), jnp.float32, -2.0, 2.0), -2.0, 2.0)
    template_slot = plant(jax.random.randint(part_splits[5], (IMAGES,), 0, SLOTS), jax.random.fold_in(part_splits[5], 1), 0, SLOTS - 1).astype(jnp.int32)
    media_counts = draw_media_counts(jax.random.fold_in(jax.random.fold_in(arg_keys[7], part), 71), part)
    return dict(images=images, w_first=w_first, w_second=w_second, calib_scale=calib_scale, calib_bias=calib_bias, template_slot=template_slot, media_counts=media_counts)


HIGH = lax.Precision.HIGHEST

def unit_rows(table):
    return table * lax.rsqrt(lax.optimization_barrier(jnp.sum(table * table, axis=-1, keepdims=True)) + 1e-06)

def reference(images, w_first, w_second, calib_scale, calib_bias, template_slot, media_counts):
    owners = N_ENROL * N_PROBE
    blocks = images.reshape(owners, IMG_DEV, D_IN)

    def embed_block(block):
        hidden = jax.nn.gelu(jnp.dot(block, w_first, precision=HIGH, preferred_element_type=jnp.float32))
        feature = jnp.dot(hidden, w_second, precision=HIGH, preferred_element_type=jnp.float32)
        return unit_rows(feature)
    embedding = lax.map(embed_block, blocks).reshape(IMAGES, D_EMB)
    ends = jnp.cumsum(media_counts, axis=1).astype(jnp.int32)
    position = jnp.arange(IMG_DEV, dtype=jnp.int32)
    owner = lax.optimization_barrier(jnp.sum((ends[:, None, :] <= position[None, :, None]).astype(jnp.int32), axis=2)).reshape(IMAGES)
    owner = owner.astype(jnp.int32)
    slot = template_slot.astype(jnp.int32)
    erow = owner // N_PROBE
    pcol = owner % N_PROBE
    is_enrol = slot < ET_OWN
    enrol_index = jnp.where(is_enrol, owner * ET_OWN + slot, ENROL).astype(jnp.int32)
    probe_index = jnp.where(is_enrol, PROBE, pcol * (N_ENROL * PT_OWN) + erow * PT_OWN + slot - ET_OWN).astype(jnp.int32)
    enrol_sum = jax.ops.segment_sum(embedding, enrol_index, num_segments=ENROL + 1)[:ENROL]
    probe_sum = jax.ops.segment_sum(embedding, probe_index, num_segments=PROBE + 1)[:PROBE]
    enrol_unit = unit_rows(enrol_sum)
    probe_unit = unit_rows(probe_sum)
    cosine = jnp.dot(enrol_unit, probe_unit.T, precision=HIGH, preferred_element_type=jnp.float32)
    return jax.nn.sigmoid(calib_scale[0] * cosine + calib_bias[0]).astype(jnp.bfloat16)
```

```python
import functools

import jax
import jax.numpy as jnp
from jax import lax
from jax.experimental import pallas as pl
from jax.experimental.pallas import tpu as pltpu
from jax.sharding import PartitionSpec as P

ET_OWN = 128
PT_OWN = 64
SLOTS = ET_OWN + PT_OWN
NONE = -4096
EPS = 1e-06
LANES = 128
CHUNK = 256
F32 = jnp.float32
BF16 = jnp.bfloat16


def split(value):
    high = value.astype(BF16)
    return high, (value - high.astype(F32)).astype(BF16)


def unit(table):
    return table * lax.rsqrt(jnp.sum(table * table, axis=-1, keepdims=True) + EPS)


def dot(a, b, dims=((1,), (0,))):
    return lax.dot_general(a, b, (dims, ((), ())), preferred_element_type=F32)


def place(n_enrol, n_probe):
    z, p = lax.axis_index("enrol"), lax.axis_index("probe")
    rows, chips = n_enrol // 2, n_probe // 2
    return z // rows, (z % rows) * chips + p // 2, p % 2


def embed_kernel(n_enrol, n_probe, count, slots, images, w_first, w_second, *rest):
    chips = n_enrol * n_probe // 4
    owners = n_enrol * n_probe
    far, near = rest[:chips], rest[chips : 2 * chips]
    (img, w1, w2, emb, table, ends, sem_img, sem_w1, sem_w2) = rest[2 * chips :]
    n_img, d_in = images.shape
    width = w_second.shape[1]
    pieces = w1.shape[0]
    block = near[0].shape[0]
    copy_img = pltpu.make_async_copy(images, img, sem_img)
    copy_img.start()
    copies = []
    for j in range(pieces):
        a = pltpu.make_async_copy(w_first.at[:, pl.ds(j * CHUNK, CHUNK)], w1.at[j], sem_w1.at[j])
        b = pltpu.make_async_copy(w_second.at[pl.ds(j * CHUNK, CHUNK)], w2.at[j], sem_w2.at[j])
        a.start()
        b.start()
        copies.append((a, b))

    ends[0] = 0
    rows = slots.shape[0]
    position = lax.broadcasted_iota(jnp.int32, (rows, LANES), 0) * LANES
    position = position + lax.broadcasted_iota(jnp.int32, (rows, LANES), 1)
    odd = jnp.zeros((rows, LANES), jnp.int32)
    total = jnp.int32(0)
    for o in range(owners):
        total = total + count[0, o]
        ends[o + 1] = total
        odd = jnp.where(position >= total, (o + 1) % 2, odd)
    table[...] = jnp.full(table.shape, NONE, jnp.int32)
    table[0:rows, :] = slots[...] + SLOTS * odd

    copy_img.wait()
    x_high, x_low = split(img[...])
    feature = jnp.zeros((n_img, width), F32)
    for j in range(pieces):
        copies[j][0].wait()
        w_high, w_low = split(w1[j])
        pre = dot(x_high, w_high) + dot(x_low, w_high) + dot(x_high, w_low)
        h_high, h_low = split(jax.nn.gelu(pre))
        copies[j][1].wait()
        v_high, v_low = split(w2[j])
        feature = feature + (dot(h_high, v_high) + dot(h_low, v_high) + dot(h_high, v_low))
    feature = unit(feature)
    tiles = width // LANES
    for t in range(tiles):
        emb[t, 0:n_img, :] = feature[:, t * LANES : (t + 1) * LANES]
        emb[t, n_img : n_img + block, :] = jnp.zeros((block, LANES), F32)

    half, chip, _ = place(n_enrol, n_probe)
    lane = lax.broadcasted_iota(jnp.int32, (1, LANES), 1)

    def window(start, size):
        row, shift = start // LANES, start % LANES
        back = (LANES - shift) % LANES
        one = pltpu.roll(table[pl.ds(row, 1), :], back, 1)
        two = pltpu.roll(table[pl.ds(row + 1, 1), :], back, 1)
        ids = jnp.where(lane < LANES - shift, one, two)
        return jnp.where(lane < size, ids, NONE).astype(F32)

    for k in range(chips):
        to = chip ^ k
        for side in range(2):
            pair = (half if side else 1 - half) * chips + to
            start, stop = ends[2 * pair], ends[2 * pair + 2]
            out = near[k] if side else far[k]
            for t in range(tiles):
                out[0:block, t * LANES : (t + 1) * LANES] = emb[t, pl.ds(start, block), :]
            far[k][block + side : block + side + 1, 0:LANES] = window(start, stop - start)


def embed(n_enrol, n_probe, images, w_first, w_second, slots, count):
    chips = n_enrol * n_probe // 4
    n_img, d_in = images.shape
    width = w_second.shape[1]
    pieces = w_second.shape[0] // CHUNK
    block = 4 * n_img // (n_enrol * n_probe)
    vmem = pl.BlockSpec(memory_space=pltpu.VMEM)
    hbm = pl.BlockSpec(memory_space=pl.ANY)
    outs = pl.pallas_call(
        functools.partial(embed_kernel, n_enrol, n_probe),
        out_shape=[jax.ShapeDtypeStruct((block + 8, width), F32)] * chips
        + [jax.ShapeDtypeStruct((block, width), F32)] * chips,
        in_specs=[pl.BlockSpec(memory_space=pltpu.SMEM), vmem, hbm, hbm, hbm],
        out_specs=[vmem] * (2 * chips),
        scratch_shapes=[
            pltpu.VMEM((n_img, d_in), F32),
            pltpu.VMEM((pieces, d_in, CHUNK), F32),
            pltpu.VMEM((pieces, CHUNK, width), F32),
            pltpu.VMEM((width // LANES, n_img + block, LANES), F32),
            pltpu.VMEM((n_img // LANES + 8 - n_img // LANES % 8, LANES), jnp.int32),
            pltpu.SMEM((n_enrol * n_probe + 1,), jnp.int32),
            pltpu.SemaphoreType.DMA,
            pltpu.SemaphoreType.DMA((pieces,)),
            pltpu.SemaphoreType.DMA((pieces,)),
        ],
        compiler_params=pltpu.CompilerParams(vmem_limit_bytes=24 << 20),
        name="embed",
    )(count, slots.reshape(n_img // LANES, LANES), images, w_first, w_second)
    return outs[:chips], outs[chips:]


def pool_kernel(n_enrol, n_probe, side, *refs):
    chips = n_enrol * n_probe // 4
    rows, ids = refs[:chips], refs[chips : 2 * chips]
    mine, other = refs[2 * chips :]
    _, _, core = place(n_enrol, n_probe)
    block = rows[0].shape[0] - (0 if side else 8)
    first = block - 0
    slot = lax.broadcasted_iota(jnp.int32, (2 * SLOTS, block), 0)
    total = jnp.zeros((2 * SLOTS, mine.shape[1]), F32)
    for k in range(chips):
        at = first + side
        want = ids[k][at : at + 1, 0:LANES][:, :block].astype(jnp.int32)
        moved = want - core * SLOTS
        want = jnp.where((want >= 0) & (moved < 0), moved + 2 * SLOTS, moved)
        pick = (slot == want).astype(F32).astype(BF16)
        high, low = split(rows[k][0:block, :])
        total = total + dot(pick, high) + dot(pick, low)
    mine[...] = total[:SLOTS]
    other[...] = total[SLOTS:]


def pool(n_enrol, n_probe, side, rows, ids):
    width = rows[0].shape[1]
    vmem = pl.BlockSpec(memory_space=pltpu.VMEM)
    return pl.pallas_call(
        functools.partial(pool_kernel, n_enrol, n_probe, side),
        out_shape=[jax.ShapeDtypeStruct((SLOTS, width), F32)] * 2,
        in_specs=[vmem] * (2 * len(rows)),
        out_specs=[vmem] * 2,
        compiler_params=pltpu.CompilerParams(vmem_limit_bytes=8 << 20),
        name="pool_near" if side else "pool_far",
    )(*rows, *ids)


def score_kernel(n_enrol, n_probe, scale, bias, *refs):
    rows, cols = n_enrol // 2, n_probe // 2
    enrol, probe = refs[: 2 * cols], refs[2 * cols : 2 * cols + rows]
    out, table = refs[2 * cols + rows :]
    z, p = lax.axis_index("enrol"), lax.axis_index("probe")
    for k in range(rows):
        own = (z ^ k) * PT_OWN
        across = (z ^ k ^ rows) * PT_OWN
        table[pl.ds(pl.multiple_of(own, PT_OWN), PT_OWN), :] = unit(probe[k][0:PT_OWN, :])
        table[pl.ds(pl.multiple_of(across, PT_OWN), PT_OWN), :] = unit(probe[k][PT_OWN:, :])
    p_high, p_low = split(table[...])
    slope, offset = scale[0], bias[0]
    last = ((1,), (1,))
    for k in range(n_probe):
        e_high, e_low = split(unit(enrol[k][...]))
        cosine = dot(e_high, p_high, last) + dot(e_low, p_high, last) + dot(e_high, p_low, last)
        at = pl.multiple_of((p ^ k) * ET_OWN, ET_OWN)
        out[pl.ds(at, ET_OWN), :] = jax.nn.sigmoid(slope * cosine + offset).astype(BF16)


def score(n_enrol, n_probe, scale, bias, enrol, probe):
    width = enrol[0].shape[1]
    vmem = pl.BlockSpec(memory_space=pltpu.VMEM)
    smem = pl.BlockSpec(memory_space=pltpu.SMEM)
    return pl.pallas_call(
        functools.partial(score_kernel, n_enrol, n_probe),
        out_shape=jax.ShapeDtypeStruct((n_probe * ET_OWN, n_enrol * PT_OWN), BF16),
        in_specs=[smem, smem] + [vmem] * (len(enrol) + len(probe)),
        out_specs=vmem,
        scratch_shapes=[pltpu.VMEM((n_enrol * PT_OWN, width), F32)],
        compiler_params=pltpu.CompilerParams(vmem_limit_bytes=8 << 20),
        name="score",
    )(scale, bias, *enrol, *probe)


def solution(mesh):
    n_enrol, n_probe = mesh.shape["enrol"], mesh.shape["probe"]
    rows, cols = n_enrol // 2, n_probe // 2
    chips = rows * cols

    def flip(value, enrol_bits, probe_bits):
        pairs = [
            (z * n_probe + p, (z ^ enrol_bits) * n_probe + (p ^ probe_bits))
            for z in range(n_enrol)
            for p in range(n_probe)
        ]
        return lax.ppermute(value, ("enrol", "probe"), pairs)

    def across_chips(blocks):
        return [blocks[0]] + [
            flip(blocks[k], k // cols, 2 * (k % cols)) for k in range(1, chips)
        ]

    def shards(images, w_first, w_second, scale, bias, template_slot, media_counts):
        far, near = embed(n_enrol, n_probe, images, w_first, w_second, template_slot, media_counts)
        far = across_chips(far)
        near = across_chips(near)
        mine, other = pool(n_enrol, n_probe, 0, far, far)
        far_sum = mine + flip(other, 0, 1)
        from_far = flip(far_sum, rows, 0)
        mine, other = pool(n_enrol, n_probe, 1, near, far)
        near_sum = mine + flip(other, 0, 1)
        probe_far = flip(near_sum[ET_OWN:], rows, 0)
        own = near_sum + from_far
        probe = jnp.concatenate([own[ET_OWN:], far_sum[ET_OWN:] + probe_far])
        enrol = own[:ET_OWN]
        probe_parts = [probe] + [flip(probe, k, 0) for k in range(1, rows)]
        enrol_parts = []
        for k in range(cols):
            part = flip(enrol, 0, 2 * k) if k else enrol
            enrol_parts += [part, flip(part, 0, 1)]
        return score(n_enrol, n_probe, scale, bias, enrol_parts, probe_parts)

    return jax.shard_map(
        shards,
        mesh=mesh,
        in_specs=(
            P(("groups", "enrol", "probe"), None),
            P(),
            P(),
            P(),
            P(),
            P(("groups", "enrol", "probe")),
            P(("groups", "enrol", "probe"), None),
        ),
        out_specs=P(("groups", "enrol"), "probe"),
        check_vma=False,
    )
```

```python
import functools
import math

import jax
import jax.numpy as jnp
from jax import lax
from jax.experimental import pallas as pl
from jax.experimental.pallas import tpu as pltpu
from jax.sharding import PartitionSpec as P


ET_OWN = 128
PT_OWN = 64
SLOTS = ET_OWN + PT_OWN
NONE = -4096
EPS = 1e-06
LANES = 128
CHUNK = 256
PIECE = 32
F32 = jnp.float32
BF16 = jnp.bfloat16
ROOT = math.sqrt(2.0 / math.pi)


def split(value):
    high = value.astype(BF16)
    return high, (value - high.astype(F32)).astype(BF16)


def unit(table):
    return table * lax.rsqrt(jnp.sum(table * table, axis=-1, keepdims=True) + EPS)


def dot(a, b, dims=((1,), (0,))):
    return lax.dot_general(a, b, (dims, ((), ())), preferred_element_type=F32)


def place(n_enrol, n_probe):
    z, p = lax.axis_index("enrol"), lax.axis_index("probe")
    rows, chips = n_enrol // 2, n_probe // 2
    return z // rows, (z % rows) * chips + p // 2, p % 2


def gelu(x):
    inner = x * (ROOT + (ROOT * 0.044715) * (x * x))
    half = 0.5 * x
    return half + half * jnp.tanh(inner)


def embed_kernel(n_enrol, n_probe, count_hbm, slots_hbm, images, w_first, w_second, *rest):
    chips = n_enrol * n_probe // 4
    owners = n_enrol * n_probe
    far, near = rest[:chips], rest[chips : 2 * chips]
    (img, w1, w2, x3, w3, pre, h3, v3, feature, emb, slots, table, count, ends, sem_img, sem_w1, sem_w2, sem_small) = rest[
        2 * chips :
    ]
    n_img, d_in = images.shape
    width = w_second.shape[1]
    pieces = w1.shape[0]
    block = near[0].shape[0]
    copy_img = pltpu.make_async_copy(images, img, sem_img)
    copy_img.start()
    copies = []
    for j in range(pieces):
        a = pltpu.make_async_copy(w_first.at[:, pl.ds(j * CHUNK, CHUNK)], w1.at[j], sem_w1.at[j])
        b = pltpu.make_async_copy(w_second.at[pl.ds(j * CHUNK, CHUNK)], w2.at[j], sem_w2.at[j])
        copies.append((a, b))
    copies[0][0].start()
    small = [
        pltpu.make_async_copy(count_hbm, count, sem_small.at[0]),
        pltpu.make_async_copy(slots_hbm, slots, sem_small.at[1]),
    ]
    for copy in small:
        copy.start()
    for j in range(1, pieces):
        copies[j][0].start()
        copies[j - 1][1].start()
    copies[pieces - 1][1].start()

    copy_img.wait()
    for r in range(0, n_img, PIECE):
        at = pl.ds(r, PIECE)
        high, low = split(img[at, :])
        x3[at, 0:d_in] = high
        x3[at, d_in : 2 * d_in] = low
        x3[at, 2 * d_in :] = high

    def thrice(source, target, rows):
        for r in range(0, rows, PIECE):
            high, low = split(source[pl.ds(r, PIECE), :])
            target[pl.ds(r, PIECE), :] = high
            target[pl.ds(rows + r, PIECE), :] = high
            target[pl.ds(2 * rows + r, PIECE), :] = low

    def load(j):
        copies[j][0].wait()
        thrice(w1.at[j], w3.at[j % 2], d_in)

    load(0)
    pre[0] = dot(x3[...], w3[0])
    load(1)

    def trip(i, carry):
        for s in range(2):
            j = 2 * i + s
            for r in range(0, n_img, PIECE):
                at = pl.ds(r, PIECE)
                high, low = split(gelu(pre[s, at, :]))
                h3[s, at, 0:CHUNK] = high
                h3[s, at, CHUNK : 2 * CHUNK] = low
                h3[s, at, 2 * CHUNK :] = high
            pre[1 - s] = dot(x3[...], w3[1 - s])
            thrice(w1.at[jnp.minimum(j + 2, pieces - 1)], w3.at[s], d_in)
            thrice(w2.at[j], v3.at[s], CHUNK)
            feature[...] = feature[...] + dot(h3[s], v3[s])
        return carry

    for j in range(pieces):
        if j > 1:
            copies[j][0].wait()
        copies[j][1].wait()
    feature[...] = jnp.zeros_like(feature)
    lax.fori_loop(0, pieces // 2, trip, 0)

    for copy in small:
        copy.wait()
    ends[0] = 0
    rows = slots.shape[0]
    position = lax.broadcasted_iota(jnp.int32, (rows, LANES), 0) * LANES
    position = position + lax.broadcasted_iota(jnp.int32, (rows, LANES), 1)
    odd = jnp.zeros((rows, LANES), jnp.int32)
    total = jnp.int32(0)
    for o in range(owners):
        total = total + count[0, o]
        ends[o + 1] = total
        odd = jnp.where(position >= total, (o + 1) % 2, odd)
    table[...] = jnp.full(table.shape, NONE, jnp.int32)
    table[0:rows, :] = slots[...] + SLOTS * odd

    tiles = width // LANES
    for r in range(0, n_img, PIECE):
        rows = unit(feature[pl.ds(r, PIECE), :])
        for t in range(tiles):
            emb[t, pl.ds(r, PIECE), :] = rows[:, t * LANES : (t + 1) * LANES]
    for t in range(tiles):
        emb[t, n_img : n_img + block, :] = jnp.zeros((block, LANES), F32)

    half, chip, _ = place(n_enrol, n_probe)
    lane = lax.broadcasted_iota(jnp.int32, (1, LANES), 1)

    def window(start, size):
        row, shift = start // LANES, start % LANES
        back = (LANES - shift) % LANES
        one = pltpu.roll(table[pl.ds(row, 1), :], back, 1)
        two = pltpu.roll(table[pl.ds(row + 1, 1), :], back, 1)
        ids = jnp.where(lane < LANES - shift, one, two)
        return jnp.where(lane < size, ids, NONE).astype(F32)

    for k in range(chips):
        to = chip ^ k
        for side in range(2):
            pair = (half if side else 1 - half) * chips + to
            start, stop = ends[2 * pair], ends[2 * pair + 2]
            out = near[k] if side else far[k]
            for t in range(tiles):
                out[0:block, t * LANES : (t + 1) * LANES] = emb[t, pl.ds(start, block), :]
            far[k][block + side : block + side + 1, 0:LANES] = window(start, stop - start)


def embed(n_enrol, n_probe, images, w_first, w_second, slots, count):
    chips = n_enrol * n_probe // 4
    n_img, d_in = images.shape
    width = w_second.shape[1]
    pieces = w_second.shape[0] // CHUNK
    block = 4 * n_img // (n_enrol * n_probe)
    vmem = pl.BlockSpec(memory_space=pltpu.VMEM)
    hbm = pl.BlockSpec(memory_space=pltpu.HBM)
    outs = pl.pallas_call(
        functools.partial(embed_kernel, n_enrol, n_probe),
        out_shape=[jax.ShapeDtypeStruct((block + 8, width), F32)] * chips
        + [jax.ShapeDtypeStruct((block, width), F32)] * chips,
        in_specs=[hbm] * 5,
        out_specs=[vmem] * (2 * chips),
        scratch_shapes=[
            pltpu.VMEM((n_img, d_in), F32),
            pltpu.VMEM((pieces, d_in, CHUNK), F32),
            pltpu.VMEM((pieces, CHUNK, width), F32),
            pltpu.VMEM((n_img, 3 * d_in), BF16),
            pltpu.VMEM((2, 3 * d_in, CHUNK), BF16),
            pltpu.VMEM((2, n_img, CHUNK), F32),
            pltpu.VMEM((2, n_img, 3 * CHUNK), BF16),
            pltpu.VMEM((2, 3 * CHUNK, width), BF16),
            pltpu.VMEM((n_img, width), F32),
            pltpu.VMEM((width // LANES, n_img + block, LANES), F32),
            pltpu.VMEM((n_img // LANES, LANES), jnp.int32),
            pltpu.VMEM((n_img // LANES + 8 - n_img // LANES % 8, LANES), jnp.int32),
            pltpu.SMEM((1, n_enrol * n_probe), jnp.int32),
            pltpu.SMEM((n_enrol * n_probe + 1,), jnp.int32),
            pltpu.SemaphoreType.DMA,
            pltpu.SemaphoreType.DMA((pieces,)),
            pltpu.SemaphoreType.DMA((pieces,)),
            pltpu.SemaphoreType.DMA((2,)),
        ],
        compiler_params=pltpu.CompilerParams(vmem_limit_bytes=67043328 - (1280 << 10)),
        name="embed",
    )(count, slots.reshape(n_img // LANES, LANES), images, w_first, w_second)
    return outs[:chips], outs[chips:]


def picked(core, ids, side, rows):
    block = rows.shape[0] if side else rows.shape[0] - 8
    at = ids.shape[0] - 8 + side
    want = ids[at : at + 1, 0:LANES][:, :block].astype(jnp.int32)
    moved = want - core * SLOTS
    want = jnp.where((want >= 0) & (moved < 0), moved + 2 * SLOTS, moved)
    slot = lax.broadcasted_iota(jnp.int32, (2 * SLOTS, block), 0)
    pick = (slot == want).astype(F32).astype(BF16)
    high, low = split(rows[0:block, :])
    return dot(pick, high) + dot(pick, low)


def pool_own_kernel(far, near, far_mine, far_other, near_mine, near_other):
    core = lax.axis_index("probe") % 2
    sums = picked(core, far, 0, far)
    far_mine[...], far_other[...] = sums[:SLOTS], sums[SLOTS:]
    sums = picked(core, far, 1, near)
    near_mine[...], near_other[...] = sums[:SLOTS], sums[SLOTS:]


def pool_kernel(side, count, *refs):
    ids, rows = refs[:count], refs[count : 2 * count] if side else refs[:count]
    mine_before, other_before, mine, other = refs[-4:]
    core = lax.axis_index("probe") % 2
    sums = picked(core, ids[0], side, rows[0])
    for k in range(1, count):
        sums = sums + picked(core, ids[k], side, rows[k])
    mine[...] = sums[:SLOTS] + mine_before[...]
    other[...] = sums[SLOTS:] + other_before[...]


def local(kernel, outs, *args, limit=8 << 20):
    vmem = pl.BlockSpec(memory_space=pltpu.VMEM)
    return pl.pallas_call(
        kernel,
        out_shape=[jax.ShapeDtypeStruct(shape, F32) for shape in outs],
        in_specs=[vmem] * len(args),
        out_specs=[vmem] * len(outs),
        compiler_params=pltpu.CompilerParams(vmem_limit_bytes=limit),
    )(*args)


def add_kernel(a, b, out):
    out[...] = a[...] + b[...]


def score_kernel(n_enrol, n_probe, scale, bias, *refs):
    rows, cols = n_enrol // 2, n_probe // 2
    enrol, probe = refs[: 2 * cols], refs[2 * cols : 2 * cols + rows]
    out, table = refs[2 * cols + rows :]
    z, p = lax.axis_index("enrol"), lax.axis_index("probe")
    for k in range(rows):
        own = (z ^ k) * PT_OWN
        across = (z ^ k ^ rows) * PT_OWN
        table[pl.ds(pl.multiple_of(own, PT_OWN), PT_OWN), :] = unit(probe[k][0:PT_OWN, :])
        table[pl.ds(pl.multiple_of(across, PT_OWN), PT_OWN), :] = unit(probe[k][PT_OWN:, :])
    p_high, p_low = split(table[...])
    slope, offset = scale[0], bias[0]
    last = ((1,), (1,))
    for k in range(n_probe):
        e_high, e_low = split(unit(enrol[k][...]))
        cosine = dot(e_high, p_high, last) + dot(e_low, p_high, last) + dot(e_high, p_low, last)
        at = pl.multiple_of((p ^ k) * ET_OWN, ET_OWN)
        out[pl.ds(at, ET_OWN), :] = jax.nn.sigmoid(slope * cosine + offset).astype(BF16)


def score(n_enrol, n_probe, scale, bias, enrol, probe):
    width = enrol[0].shape[1]
    vmem = pl.BlockSpec(memory_space=pltpu.VMEM)
    smem = pl.BlockSpec(memory_space=pltpu.SMEM)
    return pl.pallas_call(
        functools.partial(score_kernel, n_enrol, n_probe),
        out_shape=jax.ShapeDtypeStruct((n_probe * ET_OWN, n_enrol * PT_OWN), BF16),
        in_specs=[smem, smem] + [vmem] * (len(enrol) + len(probe)),
        out_specs=vmem,
        scratch_shapes=[pltpu.VMEM((n_enrol * PT_OWN, width), F32)],
        compiler_params=pltpu.CompilerParams(vmem_limit_bytes=8 << 20),
        name="score",
    )(scale, bias, *enrol, *probe)


def solution(mesh):
    n_enrol, n_probe = mesh.shape["enrol"], mesh.shape["probe"]
    rows, cols = n_enrol // 2, n_probe // 2
    chips = rows * cols

    def flip(value, enrol_bits, probe_bits):
        pairs = [
            (z * n_probe + p, (z ^ enrol_bits) * n_probe + (p ^ probe_bits))
            for z in range(n_enrol)
            for p in range(n_probe)
        ]
        return lax.ppermute(value, ("enrol", "probe"), pairs)

    def across_chips(blocks):
        return [flip(blocks[k], k // cols, 2 * (k % cols)) for k in range(1, chips)]

    def body(images, w_first, w_second, scale, bias, template_slot, media_counts):
        far, near = embed(n_enrol, n_probe, images, w_first, w_second, template_slot, media_counts)
        sums = (SLOTS, w_second.shape[1])
        far_in = across_chips(far)
        near_in = across_chips(near)
        far_mine, far_other, near_mine, near_other = local(
            pool_own_kernel, [sums] * 4, far[0], near[0]
        )
        kernel = functools.partial(pool_kernel, 0, chips - 1)
        far_mine, far_other = local(kernel, [sums] * 2, *far_in, far_mine, far_other)
        far_sum = far_mine + flip(far_other, 0, 1)
        from_far = flip(far_sum, rows, 0)
        kernel = functools.partial(pool_kernel, 1, chips - 1)
        near_mine, near_other = local(kernel, [sums] * 2, *far_in, *near_in, near_mine, near_other)
        near_other = flip(near_other, 0, 1)
        near_probe = near_mine[ET_OWN:] + near_other[ET_OWN:]
        probe_far = flip(near_probe, rows, 0)
        (near_sum,) = local(add_kernel, [sums], near_mine, near_other)
        own = near_sum + from_far
        probe = jnp.concatenate([own[ET_OWN:], far_sum[ET_OWN:] + probe_far])
        enrol = own[:ET_OWN]
        probe_parts = [probe] + [flip(probe, k, 0) for k in range(1, rows)]
        enrol_parts = []
        for k in range(cols):
            part = flip(enrol, 0, 2 * k) if k else enrol
            enrol_parts += [part, flip(part, 0, 1)]
        return score(n_enrol, n_probe, scale, bias, enrol_parts, probe_parts)

    return jax.shard_map(
        body,
        mesh=mesh,
        in_specs=(
            P(("groups", "enrol", "probe"), None),
            P(),
            P(),
            P(),
            P(),
            P(("groups", "enrol", "probe")),
            P(("groups", "enrol", "probe"), None),
        ),
        out_specs=P(("groups", "enrol"), "probe"),
        check_vma=False,
    )
```

```python
import functools
import math

import jax
import jax.numpy as jnp
from jax import lax
from jax.experimental import pallas as pl
from jax.experimental.pallas import tpu as pltpu
from jax.sharding import PartitionSpec as P


ET_OWN = 128
PT_OWN = 64
SLOTS = ET_OWN + PT_OWN
NONE = -4096
EPS = 1e-06
LANES = 128
CHUNK = 256
PIECE = 32
PER_TRIP = 4
F32 = jnp.float32
BF16 = jnp.bfloat16
ROOT = math.sqrt(2.0 / math.pi)


def split(value):
    high = value.astype(BF16)
    return high, (value - high.astype(F32)).astype(BF16)


def unit(table):
    return table * lax.rsqrt(jnp.sum(table * table, axis=-1, keepdims=True) + EPS)


def dot(a, b, dims=((1,), (0,))):
    return lax.dot_general(a, b, (dims, ((), ())), preferred_element_type=F32)


def place(n_enrol, n_probe):
    z, p = lax.axis_index("enrol"), lax.axis_index("probe")
    rows, chips = n_enrol // 2, n_probe // 2
    return z // rows, (z % rows) * chips + p // 2, p % 2


def gelu(x):
    inner = x * (ROOT + (ROOT * 0.044715) * (x * x))
    half = 0.5 * x
    return half + half * jnp.tanh(inner)


def embed_kernel(n_enrol, n_probe, count_hbm, slots_hbm, images, w_first, w_second, *rest):
    chips = n_enrol * n_probe // 4
    owners = n_enrol * n_probe
    far, near = rest[:chips], rest[chips : 2 * chips]
    (img, w1, w2, x3, w3, pre, h3, v3, feature, emb, slots, table, count, ends, sem_img, sem_w1, sem_w2, sem_small) = rest[
        2 * chips :
    ]
    n_img, d_in = images.shape
    width = w_second.shape[1]
    pieces = w1.shape[0]
    block = near[0].shape[0]
    copy_img = pltpu.make_async_copy(images, img, sem_img)
    copy_img.start()
    copies = []
    for j in range(pieces):
        a = pltpu.make_async_copy(w_first.at[:, pl.ds(j * CHUNK, CHUNK)], w1.at[j], sem_w1.at[j])
        b = pltpu.make_async_copy(w_second.at[pl.ds(j * CHUNK, CHUNK)], w2.at[j], sem_w2.at[j])
        copies.append((a, b))
    copies[0][0].start()
    small = [
        pltpu.make_async_copy(count_hbm, count, sem_small.at[0]),
        pltpu.make_async_copy(slots_hbm, slots, sem_small.at[1]),
    ]
    for copy in small:
        copy.start()
    for j in range(1, pieces):
        copies[j][0].start()
        copies[j - 1][1].start()
    copies[pieces - 1][1].start()

    def thrice(source, target, rows):
        for r in range(0, rows, PIECE):
            high, low = split(source[pl.ds(r, PIECE), :])
            target[pl.ds(r, PIECE), :] = high
            target[pl.ds(rows + r, PIECE), :] = high
            target[pl.ds(2 * rows + r, PIECE), :] = low

    def first(s):
        pre[s] = dot(x3[...], w3[s])

    def load(j, s):
        thrice(w1.at[j], w3.at[s], d_in)

    def bent(s, r):
        return split(gelu(pre[s, pl.ds(r, PIECE), :]))

    copy_img.wait()
    for r in range(0, n_img, PIECE):
        at = pl.ds(r, PIECE)
        high, low = split(img[at, :])
        x3[at, 0:d_in] = high
        x3[at, d_in : 2 * d_in] = low
        x3[at, 2 * d_in :] = high
    copies[0][0].wait()
    copies[1][0].wait()
    load(0, 0)
    first(0)
    load(1, 1)
    feature[...] = jnp.zeros_like(feature)

    def trip(i, carry):
        for step in range(PER_TRIP):
            j, s = PER_TRIP * i + step, step % 2
            for r in range(0, n_img, PIECE):
                at = pl.ds(r, PIECE)
                high, low = bent(s, r)
                h3[s, at, 0:CHUNK] = high
                h3[s, at, CHUNK : 2 * CHUNK] = low
                h3[s, at, 2 * CHUNK :] = high
            first(1 - s)
            load(jnp.minimum(j + 2, pieces - 1), s)
            thrice(w2.at[j], v3.at[s], CHUNK)
            feature[...] = feature[...] + dot(h3[s], v3[s])
        return carry

    for j in range(pieces):
        if j > 1:
            copies[j][0].wait()
        copies[j][1].wait()
    lax.fori_loop(0, pieces // PER_TRIP, trip, 0)

    for copy in small:
        copy.wait()
    ends[0] = 0
    rows = slots.shape[0]
    position = lax.broadcasted_iota(jnp.int32, (rows, LANES), 0) * LANES
    position = position + lax.broadcasted_iota(jnp.int32, (rows, LANES), 1)
    odd = jnp.zeros((rows, LANES), jnp.int32)
    total = jnp.int32(0)
    for o in range(owners):
        total = total + count[0, o]
        ends[o + 1] = total
        odd = jnp.where(position >= total, (o + 1) % 2, odd)
    table[...] = jnp.full(table.shape, NONE, jnp.int32)
    table[0:rows, :] = slots[...] + SLOTS * odd

    tiles = width // LANES
    for r in range(0, n_img, PIECE):
        rows = unit(feature[pl.ds(r, PIECE), :])
        for t in range(tiles):
            emb[t, pl.ds(r, PIECE), :] = rows[:, t * LANES : (t + 1) * LANES]
    for t in range(tiles):
        emb[t, n_img : n_img + block, :] = jnp.zeros((block, LANES), F32)

    half, chip, _ = place(n_enrol, n_probe)
    lane = lax.broadcasted_iota(jnp.int32, (1, LANES), 1)

    def window(start, size):
        row, shift = start // LANES, start % LANES
        back = (LANES - shift) % LANES
        one = pltpu.roll(table[pl.ds(row, 1), :], back, 1)
        two = pltpu.roll(table[pl.ds(row + 1, 1), :], back, 1)
        ids = jnp.where(lane < LANES - shift, one, two)
        return jnp.where(lane < size, ids, NONE).astype(F32)

    for k in range(chips):
        to = chip ^ k
        for side in range(2):
            pair = (half if side else 1 - half) * chips + to
            start, stop = ends[2 * pair], ends[2 * pair + 2]
            out = near[k] if side else far[k]
            for t in range(tiles):
                out[0:block, t * LANES : (t + 1) * LANES] = emb[t, pl.ds(start, block), :]
            far[k][block + side : block + side + 1, 0:LANES] = window(start, stop - start)


def embed(n_enrol, n_probe, images, w_first, w_second, slots, count):
    chips = n_enrol * n_probe // 4
    n_img, d_in = images.shape
    width = w_second.shape[1]
    pieces = w_second.shape[0] // CHUNK
    block = 4 * n_img // (n_enrol * n_probe)
    vmem = pl.BlockSpec(memory_space=pltpu.VMEM)
    hbm = pl.BlockSpec(memory_space=pltpu.HBM)
    inputs = count, slots.reshape(n_img // LANES, LANES), images, w_first, w_second
    outs = pl.pallas_call(
        functools.partial(embed_kernel, n_enrol, n_probe),
        out_shape=[jax.ShapeDtypeStruct((block + 8, width), F32)] * chips
        + [jax.ShapeDtypeStruct((block, width), F32)] * chips,
        in_specs=[hbm] * 5,
        out_specs=[vmem] * (2 * chips),
        scratch_shapes=[
            pltpu.VMEM((n_img, d_in), F32),
            pltpu.VMEM((pieces, d_in, CHUNK), F32),
            pltpu.VMEM((pieces, CHUNK, width), F32),
            pltpu.VMEM((n_img, 3 * d_in), BF16),
            pltpu.VMEM((2, 3 * d_in, CHUNK), BF16),
            pltpu.VMEM((2, n_img, CHUNK), F32),
            pltpu.VMEM((2, n_img, 3 * CHUNK), BF16),
            pltpu.VMEM((2, 3 * CHUNK, width), BF16),
            pltpu.VMEM((n_img, width), F32),
            pltpu.VMEM((width // LANES, n_img + block, LANES), F32),
            pltpu.VMEM((n_img // LANES, LANES), jnp.int32),
            pltpu.VMEM((n_img // LANES + 8 - n_img // LANES % 8, LANES), jnp.int32),
            pltpu.SMEM((1, n_enrol * n_probe), jnp.int32),
            pltpu.SMEM((n_enrol * n_probe + 1,), jnp.int32),
            pltpu.SemaphoreType.DMA,
            pltpu.SemaphoreType.DMA((pieces,)),
            pltpu.SemaphoreType.DMA((pieces,)),
            pltpu.SemaphoreType.DMA((2,)),
        ],
        compiler_params=pltpu.CompilerParams(vmem_limit_bytes=52 << 20),
        name="embed",
    )(*[pltpu.with_memory_space_constraint(x, pltpu.HBM) for x in inputs])
    return outs[:chips], outs[chips:]


def picked(core, ids, side, rows):
    block = rows.shape[0] if side else rows.shape[0] - 8
    at = ids.shape[0] - 8 + side
    want = ids[at : at + 1, 0:LANES][:, :block].astype(jnp.int32)
    moved = want - core * SLOTS
    want = jnp.where((want >= 0) & (moved < 0), moved + 2 * SLOTS, moved)
    slot = lax.broadcasted_iota(jnp.int32, (2 * SLOTS, block), 0)
    pick = (slot == want).astype(F32).astype(BF16)
    high, low = split(rows[0:block, :])
    return dot(pick, high) + dot(pick, low)


def pool_own_kernel(side, ids, rows, mine, other):
    sums = picked(lax.axis_index("probe") % 2, ids, side, rows)
    mine[...], other[...] = sums[:SLOTS], sums[SLOTS:]


def pool_one_kernel(half, ids, rows, out):
    sums = picked(lax.axis_index("probe") % 2, ids, 1, rows)
    out[...] = sums[SLOTS:] if half else sums[:SLOTS]


def pool_kernel(side, count, *refs):
    ids, rows = refs[:count], refs[count : 2 * count] if side else refs[:count]
    mine_before, other_before, mine, other = refs[-4:]
    core = lax.axis_index("probe") % 2
    sums = picked(core, ids[0], side, rows[0])
    for k in range(1, count):
        sums = sums + picked(core, ids[k], side, rows[k])
    mine[...] = sums[:SLOTS] + mine_before[...]
    other[...] = sums[SLOTS:] + other_before[...]


def local(kernel, outs, *args, limit=8 << 20):
    vmem = pl.BlockSpec(memory_space=pltpu.VMEM)
    return pl.pallas_call(
        kernel,
        out_shape=[jax.ShapeDtypeStruct(shape, F32) for shape in outs],
        in_specs=[vmem] * len(args),
        out_specs=[vmem] * len(outs),
        compiler_params=pltpu.CompilerParams(vmem_limit_bytes=limit),
    )(*args)


def add_kernel(a, b, out):
    out[...] = a[...] + b[...]


def score_kernel(n_enrol, n_probe, scale, bias, *refs):
    rows, cols = n_enrol // 2, n_probe // 2
    enrol, probe = refs[: 2 * cols], refs[2 * cols : 2 * cols + rows]
    out, e3, p3 = refs[2 * cols + rows :]
    width = enrol[0].shape[1]
    z, p = lax.axis_index("enrol"), lax.axis_index("probe")

    def put(table, start, size, high_low):
        at = pl.ds(pl.multiple_of(start * size, size), size)
        for t, part in enumerate(high_low):
            table[at, t * width : (t + 1) * width] = part

    for k in range(rows):
        for side in range(2):
            part = probe[k][side * PT_OWN : (side + 1) * PT_OWN, :]
            high, low = split(unit(part))
            put(p3, z ^ k ^ (side * rows), PT_OWN, (high, high, low))
    for k in range(n_probe):
        high, low = split(unit(enrol[k][...]))
        put(e3, p ^ k, ET_OWN, (high, low, high))
    cosine = dot(e3[...], p3[...], ((1,), (1,)))
    out[...] = jax.nn.sigmoid(scale[0] * cosine + bias[0]).astype(BF16)


def score(n_enrol, n_probe, scale, bias, enrol, probe):
    width = enrol[0].shape[1]
    vmem = pl.BlockSpec(memory_space=pltpu.VMEM)
    smem = pl.BlockSpec(memory_space=pltpu.SMEM)
    return pl.pallas_call(
        functools.partial(score_kernel, n_enrol, n_probe),
        out_shape=jax.ShapeDtypeStruct((n_probe * ET_OWN, n_enrol * PT_OWN), BF16),
        in_specs=[smem, smem] + [vmem] * (len(enrol) + len(probe)),
        out_specs=vmem,
        scratch_shapes=[
            pltpu.VMEM((n_probe * ET_OWN, 3 * width), BF16),
            pltpu.VMEM((n_enrol * PT_OWN, 3 * width), BF16),
        ],
        compiler_params=pltpu.CompilerParams(vmem_limit_bytes=8 << 20),
        name="score",
    )(scale, bias, *enrol, *probe)


def solution(mesh):
    n_enrol, n_probe = mesh.shape["enrol"], mesh.shape["probe"]
    rows, cols = n_enrol // 2, n_probe // 2
    chips = rows * cols

    def flip(value, enrol_bits, probe_bits):
        pairs = [
            (z * n_probe + p, (z ^ enrol_bits) * n_probe + (p ^ probe_bits))
            for z in range(n_enrol)
            for p in range(n_probe)
        ]
        return lax.ppermute(value, ("enrol", "probe"), pairs)

    def across_chips(blocks):
        moved = []
        for k in range(1, chips):
            moved.append(flip(blocks[k], k // cols, 2 * (k % cols)))
        return moved

    def body(images, w_first, w_second, scale, bias, template_slot, media_counts):
        far, near = embed(n_enrol, n_probe, images, w_first, w_second, template_slot, media_counts)
        sums = (SLOTS, w_second.shape[1])
        far_in = across_chips(far)
        near_in = across_chips(near)
        kernel = functools.partial(pool_own_kernel, 0)
        far_mine, far_other = local(kernel, [sums] * 2, far[0], far[0])
        kernel = functools.partial(pool_one_kernel, 0)
        (near_mine,) = local(kernel, [sums], far[0], near[0])
        kernel = functools.partial(pool_one_kernel, 1)
        (near_other,) = local(kernel, [sums], far[0], near[0])
        kernel = functools.partial(pool_kernel, 0, chips - 1)
        far_mine, far_other = local(kernel, [sums] * 2, *far_in, far_mine, far_other)
        far_sum = far_mine + flip(far_other, 0, 1)
        from_far = flip(far_sum, rows, 0)
        kernel = functools.partial(pool_kernel, 1, chips - 1)
        near_mine, near_other = local(kernel, [sums] * 2, *far_in, *near_in, near_mine, near_other)
        near_other = flip(near_other, 0, 1)
        near_probe = near_mine[ET_OWN:] + near_other[ET_OWN:]
        probe_far = flip(near_probe, rows, 0)
        (near_sum,) = local(add_kernel, [sums], near_mine, near_other)
        own = near_sum + from_far
        probe = jnp.concatenate([own[ET_OWN:], far_sum[ET_OWN:] + probe_far])
        enrol = own[:ET_OWN]
        probe_parts = [probe] + [flip(probe, k, 0) for k in range(1, rows)]
        enrol_parts = []
        for k in range(cols):
            part = flip(enrol, 0, 2 * k) if k else enrol
            enrol_parts += [part, flip(part, 0, 1)]
        return score(n_enrol, n_probe, scale, bias, enrol_parts, probe_parts)

    return jax.shard_map(
        body,
        mesh=mesh,
        in_specs=(
            P(("groups", "enrol", "probe"), None),
            P(),
            P(),
            P(),
            P(),
            P(("groups", "enrol", "probe")),
            P(("groups", "enrol", "probe"), None),
        ),
        out_specs=P(("groups", "enrol"), "probe"),
        check_vma=False,
    )
```

```python
import functools
import math

import jax
import jax.numpy as jnp
from jax import lax
from jax.experimental import pallas as pl
from jax.experimental.pallas import tpu as pltpu
from jax.sharding import PartitionSpec as P


ET_OWN = 128
PT_OWN = 64
SLOTS = ET_OWN + PT_OWN
NONE = -4096
EPS = 1e-06
LANES = 128
CHUNK = 256
PIECE = 32
GROUP = 4
STARTS = (1, 1, 1, 2)
LATE = 6
F32 = jnp.float32
BF16 = jnp.bfloat16
ROOT = math.sqrt(2.0 / math.pi)


def split(value):
    high = value.astype(BF16)
    return high, (value - high.astype(F32)).astype(BF16)


def unit(table):
    return table * lax.rsqrt(jnp.sum(table * table, axis=-1, keepdims=True) + EPS)


def dot(a, b, dims=((1,), (0,))):
    return lax.dot_general(a, b, (dims, ((), ())), preferred_element_type=F32)


def place(n_enrol, n_probe):
    z, p = lax.axis_index("enrol"), lax.axis_index("probe")
    rows, chips = n_enrol // 2, n_probe // 2
    return z // rows, (z % rows) * chips + p // 2, p % 2


def twice_gelu(x):
    return x + x * jnp.tanh(x * (ROOT + (ROOT * 0.044715) * (x * x)))


def embed_kernel(n_enrol, n_probe, count_hbm, slots_hbm, images, w_first, w_second, *rest):
    chips = n_enrol * n_probe // 4
    owners = n_enrol * n_probe
    far, near = rest[:chips], rest[chips : 2 * chips]
    (img, w1, w2, x3, w3, pre, h3, v3, feature, emb, slots, table, count, ends, sem_img, sem_w1, sem_w2, sem_small) = rest[
        2 * chips :
    ]
    n_img, d_in = images.shape
    width = w_second.shape[1]
    pieces = w1.shape[0]
    block = near[0].shape[0]

    def copy_first(j):
        columns = w_first.at[:, pl.ds(pl.multiple_of(j * CHUNK, CHUNK), CHUNK)]
        return pltpu.make_async_copy(columns, w1.at[j], sem_w1.at[j])

    def copy_second(j):
        part = w_second.at[pl.ds(pl.multiple_of(j * CHUNK, CHUNK), CHUNK)]
        return pltpu.make_async_copy(part, w2.at[j], sem_w2.at[j])

    quarter = n_img // 4
    image_copies = [
        pltpu.make_async_copy(
            images.at[pl.ds(q * quarter, quarter)], img.at[pl.ds(q * quarter, quarter)], sem_img.at[q]
        )
        for q in range(4)
    ]
    for copy in image_copies:
        copy.start()
    copy_first(0).start()
    queue = [copy_first(1), copy_first(2), copy_second(0)]
    for j in range(3, pieces):
        queue += [copy_first(j), copy_second(j - 2)]
    queue += [copy_second(pieces - 2), copy_second(pieces - 1)]

    def start_more(n):
        for copy in queue[:n]:
            copy.start()
        del queue[:n]

    small = [
        pltpu.make_async_copy(count_hbm, count, sem_small.at[0]),
        pltpu.make_async_copy(slots_hbm, slots, sem_small.at[1]),
    ]
    for copy in small:
        copy.start()

    def thrice(source, target, rows):
        for r in range(0, rows, PIECE):
            high, low = split(source[pl.ds(r, PIECE), :])
            target[pl.ds(r, PIECE), :] = high
            target[pl.ds(rows + r, PIECE), :] = high
            target[pl.ds(2 * rows + r, PIECE), :] = low

    def first(s):
        pre[s] = dot(x3[...], w3[s])

    def load(j, s):
        thrice(w1.at[j], w3.at[s], d_in)

    def bend(s):
        for r in range(0, n_img, PIECE):
            at = pl.ds(r, PIECE)
            high, low = split(twice_gelu(pre[s, at, :]))
            h3[s, at, 0:CHUNK] = high
            h3[s, at, CHUNK : 2 * CHUNK] = low
            h3[s, at, 2 * CHUNK :] = high

    def second(j, s):
        thrice(w2.at[j], v3.at[s], CHUNK)
        feature[...] = feature[...] + dot(h3[s], v3[s])

    for q, copy in enumerate(image_copies):
        copy.wait()
        start_more(STARTS[q])
        for r in range(q * quarter, (q + 1) * quarter, PIECE):
            at = pl.ds(r, PIECE)
            high, low = split(img[at, :])
            x3[at, 0:d_in] = high
            x3[at, d_in : 2 * d_in] = low
            x3[at, 2 * d_in :] = high
    copy_first(0).wait()
    start_more(len(queue) - LATE)
    load(0, 0)
    first(0)
    copy_first(1).wait()
    start_more(len(queue))
    load(1, 1)
    feature[...] = jnp.zeros_like(feature)

    def trip(i, carry):
        @pl.when(i == 0)
        def _():
            for j in range(GROUP):
                copy_first(j + 2).wait()
                copy_second(j).wait()

        @pl.when(i == 1)
        def _():
            for j in range(GROUP, pieces):
                if j + 2 < pieces:
                    copy_first(j + 2).wait()
                copy_second(j).wait()

        for step in range(GROUP):
            j, s = GROUP * i + step, step % 2
            bend(s)
            first(1 - s)
            load(jnp.minimum(j + 2, pieces - 1), s)
            second(j, s)
        return carry

    lax.fori_loop(0, pieces // GROUP, trip, 0)

    for copy in small:
        copy.wait()
    ends[0] = 0
    rows = slots.shape[0]
    position = lax.broadcasted_iota(jnp.int32, (rows, LANES), 0) * LANES
    position = position + lax.broadcasted_iota(jnp.int32, (rows, LANES), 1)
    odd = jnp.zeros((rows, LANES), jnp.int32)
    total = jnp.int32(0)
    for o in range(owners):
        total = total + count[0, o]
        ends[o + 1] = total
        odd = jnp.where(position >= total, (o + 1) % 2, odd)
    table[...] = jnp.full(table.shape, NONE, jnp.int32)
    table[0:rows, :] = slots[...] + SLOTS * odd

    tiles = width // LANES
    for r in range(0, n_img, PIECE):
        rows = unit(0.5 * feature[pl.ds(r, PIECE), :])
        for t in range(tiles):
            emb[t, pl.ds(r, PIECE), :] = rows[:, t * LANES : (t + 1) * LANES]
    for t in range(tiles):
        emb[t, n_img : n_img + block, :] = jnp.zeros((block, LANES), F32)

    half, chip, _ = place(n_enrol, n_probe)
    lane = lax.broadcasted_iota(jnp.int32, (1, LANES), 1)

    def window(start, size):
        row, shift = start // LANES, start % LANES
        back = (LANES - shift) % LANES
        one = pltpu.roll(table[pl.ds(row, 1), :], back, 1)
        two = pltpu.roll(table[pl.ds(row + 1, 1), :], back, 1)
        ids = jnp.where(lane < LANES - shift, one, two)
        return jnp.where(lane < size, ids, NONE).astype(F32)

    for k in range(chips):
        to = chip ^ k
        for side in range(2):
            pair = (half if side else 1 - half) * chips + to
            start, stop = ends[2 * pair], ends[2 * pair + 2]
            out = near[k] if side else far[k]
            for t in range(tiles):
                out[0:block, t * LANES : (t + 1) * LANES] = emb[t, pl.ds(start, block), :]
            far[k][block + side : block + side + 1, 0:LANES] = window(start, stop - start)


def embed(n_enrol, n_probe, images, w_first, w_second, slots, count):
    chips = n_enrol * n_probe // 4
    n_img, d_in = images.shape
    width = w_second.shape[1]
    pieces = w_second.shape[0] // CHUNK
    block = 4 * n_img // (n_enrol * n_probe)
    vmem = pl.BlockSpec(memory_space=pltpu.VMEM)
    hbm = pl.BlockSpec(memory_space=pltpu.HBM)
    inputs = count, slots.reshape(n_img // LANES, LANES), images, w_first, w_second
    outs = pl.pallas_call(
        functools.partial(embed_kernel, n_enrol, n_probe),
        out_shape=[jax.ShapeDtypeStruct((block + 8, width), F32)] * chips
        + [jax.ShapeDtypeStruct((block, width), F32)] * chips,
        in_specs=[hbm] * 5,
        out_specs=[vmem] * (2 * chips),
        scratch_shapes=[
            pltpu.VMEM((n_img, d_in), F32),
            pltpu.VMEM((pieces, d_in, CHUNK), F32),
            pltpu.VMEM((pieces, CHUNK, width), F32),
            pltpu.VMEM((n_img, 3 * d_in), BF16),
            pltpu.VMEM((2, 3 * d_in, CHUNK), BF16),
            pltpu.VMEM((2, n_img, CHUNK), F32),
            pltpu.VMEM((2, n_img, 3 * CHUNK), BF16),
            pltpu.VMEM((2, 3 * CHUNK, width), BF16),
            pltpu.VMEM((n_img, width), F32),
            pltpu.VMEM((width // LANES, n_img + block, LANES), F32),
            pltpu.VMEM((n_img // LANES, LANES), jnp.int32),
            pltpu.VMEM((n_img // LANES + 8 - n_img // LANES % 8, LANES), jnp.int32),
            pltpu.SMEM((1, n_enrol * n_probe), jnp.int32),
            pltpu.SMEM((n_enrol * n_probe + 1,), jnp.int32),
            pltpu.SemaphoreType.DMA((4,)),
            pltpu.SemaphoreType.DMA((pieces,)),
            pltpu.SemaphoreType.DMA((pieces,)),
            pltpu.SemaphoreType.DMA((2,)),
        ],
        compiler_params=pltpu.CompilerParams(vmem_limit_bytes=52 << 20),
        name="embed",
    )(*[pltpu.with_memory_space_constraint(x, pltpu.HBM) for x in inputs])
    return outs[:chips], outs[chips:]


def picked(half, ids, side, rows):
    block = rows.shape[0] if side else rows.shape[0] - 8
    at = ids.shape[0] - 8 + side
    want = ids[at : at + 1, 0:LANES][:, :block].astype(jnp.int32)
    core = lax.axis_index("probe") % 2
    want = want - (core ^ half) * SLOTS
    slot = lax.broadcasted_iota(jnp.int32, (SLOTS, block), 0)
    pick = (slot == want).astype(F32).astype(BF16)
    high, low = split(rows[0:block, :])
    return dot(pick, high) + dot(pick, low)


def pool_own_kernel(side, ids, rows, mine, other):
    mine[...] = picked(0, ids, side, rows)
    other[...] = picked(1, ids, side, rows)


def pool_one_kernel(half, ids, rows, out):
    out[...] = picked(half, ids, 1, rows)


def pool_kernel(side, half, count, *refs):
    ids, rows = refs[:count], refs[count : 2 * count] if side else refs[:count]
    before, out = refs[-2:]
    sums = before[...]
    for k in range(count):
        sums = sums + picked(half, ids[k], side, rows[k])
    out[...] = sums


def local(kernel, outs, *args, limit=8 << 20, kind=F32):
    vmem = pl.BlockSpec(memory_space=pltpu.VMEM)
    return pl.pallas_call(
        kernel,
        out_shape=[jax.ShapeDtypeStruct(shape, kind) for shape in outs],
        in_specs=[vmem] * len(args),
        out_specs=[vmem] * len(outs),
        compiler_params=pltpu.CompilerParams(vmem_limit_bytes=limit),
    )(*args)


def add_kernel(a, b, out):
    out[...] = a[...] + b[...]


def prepare_kernel(own, other, own_out, other_out):
    width = own.shape[1]
    for table, out in ((own, own_out), (other, other_out)):
        out[:, :width], out[:, width:] = split(unit(table[...]))


def score_kernel(n_enrol, n_probe, scale, bias, *refs):
    rows, cols = n_enrol // 2, n_probe // 2
    enrol, probe = refs[: 2 * cols], refs[2 * cols : 2 * cols + 2 * rows]
    out, e3, p3 = refs[2 * cols + 2 * rows :]
    width = probe[0].shape[1]
    z, p = lax.axis_index("enrol"), lax.axis_index("probe")

    def put(table, start, size, high_low):
        at = pl.ds(pl.multiple_of(start * size, size), size)
        for t, part in enumerate(high_low):
            table[at, t * width : (t + 1) * width] = part

    for k in range(rows):
        for side in range(2):
            high, low = split(unit(probe[2 * k + side][...]))
            put(p3, z ^ k ^ (side * rows), PT_OWN, (high, high, low))
    for k in range(n_probe):
        if k < 2:
            high, low = enrol[k][:, :width], enrol[k][:, width:]
        else:
            high, low = split(unit(enrol[k][...]))
        put(e3, p ^ k, ET_OWN, (high, low, high))
    cosine = dot(e3[...], p3[...], ((1,), (1,)))
    out[...] = jax.nn.sigmoid(scale[0] * cosine + bias[0]).astype(BF16)


def score(n_enrol, n_probe, scale, bias, enrol, probe):
    width = probe[0].shape[1]
    vmem = pl.BlockSpec(memory_space=pltpu.VMEM)
    smem = pl.BlockSpec(memory_space=pltpu.SMEM)
    return pl.pallas_call(
        functools.partial(score_kernel, n_enrol, n_probe),
        out_shape=jax.ShapeDtypeStruct((n_probe * ET_OWN, n_enrol * PT_OWN), BF16),
        in_specs=[smem, smem] + [vmem] * (len(enrol) + len(probe)),
        out_specs=vmem,
        scratch_shapes=[
            pltpu.VMEM((n_probe * ET_OWN, 3 * width), BF16),
            pltpu.VMEM((n_enrol * PT_OWN, 3 * width), BF16),
        ],
        compiler_params=pltpu.CompilerParams(vmem_limit_bytes=8 << 20),
        name="score",
    )(scale, bias, *enrol, *probe)


def solution(mesh):
    n_enrol, n_probe = mesh.shape["enrol"], mesh.shape["probe"]
    rows, cols = n_enrol // 2, n_probe // 2
    chips = rows * cols

    def flip(value, enrol_bits, probe_bits):
        pairs = [
            (z * n_probe + p, (z ^ enrol_bits) * n_probe + (p ^ probe_bits))
            for z in range(n_enrol)
            for p in range(n_probe)
        ]
        return lax.ppermute(value, ("enrol", "probe"), pairs)

    def across_chips(blocks):
        moved = []
        for k in range(1, chips):
            moved.append(flip(blocks[k], k // cols, 2 * (k % cols)))
        return moved

    def body(images, w_first, w_second, scale, bias, template_slot, media_counts):
        far, near = embed(n_enrol, n_probe, images, w_first, w_second, template_slot, media_counts)
        sums = (SLOTS, w_second.shape[1])
        far_in = across_chips(far)
        near_in = across_chips(near)
        kernel = functools.partial(pool_own_kernel, 0)
        far_mine, far_other = local(kernel, [sums] * 2, far[0], far[0])
        kernel = functools.partial(pool_one_kernel, 0)
        (near_mine,) = local(kernel, [sums], far[0], near[0])
        kernel = functools.partial(pool_one_kernel, 1)
        (near_other,) = local(kernel, [sums], far[0], near[0])

        def pool(side, half, *args):
            kernel = functools.partial(pool_kernel, side, half, chips - 1)
            return local(kernel, [sums], *args)[0]

        far_other = pool(0, 1, *far_in, far_other)
        far_other = flip(far_other, 0, 1)
        far_mine = pool(0, 0, *far_in, far_mine)
        far_enrol, far_probe = lax.optimization_barrier(
            (far_mine[:ET_OWN] + far_other[:ET_OWN], far_mine[ET_OWN:] + far_other[ET_OWN:])
        )
        enrol_far = flip(far_enrol, rows, 0)
        own_far = flip(far_probe, rows, 0)
        near_other = pool(1, 1, *far_in, *near_in, near_other)
        near_mine = pool(1, 0, *far_in, *near_in, near_mine)
        near_other = flip(near_other, 0, 1)
        near_probe = near_mine[ET_OWN:] + near_other[ET_OWN:]
        probe_far = flip(near_probe, rows, 0)
        (near_sum,) = local(add_kernel, [sums], near_mine, near_other)
        enrol = near_sum[:ET_OWN] + enrol_far
        own_probe = near_sum[ET_OWN:] + own_far
        across_probe = far_probe + probe_far
        probe_parts = []
        for k in range(rows):
            for part in (own_probe, across_probe):
                probe_parts.append(flip(part, k, 0) if k else part)
        pair = (ET_OWN, 2 * enrol.shape[1])
        enrol_parts = [enrol, flip(enrol, 0, 1)]
        enrol_parts = [*local(prepare_kernel, [pair] * 2, *enrol_parts, kind=BF16)]
        for k in range(1, cols):
            part = flip(enrol, 0, 2 * k)
            enrol_parts += [part, flip(part, 0, 1)]
        return score(n_enrol, n_probe, scale, bias, enrol_parts, probe_parts)

    return jax.shard_map(
        body,
        mesh=mesh,
        in_specs=(
            P(("groups", "enrol", "probe"), None),
            P(),
            P(),
            P(),
            P(),
            P(("groups", "enrol", "probe")),
            P(("groups", "enrol", "probe"), None),
        ),
        out_specs=P(("groups", "enrol"), "probe"),
        check_vma=False,
    )
```

```python
import functools
import math

import jax
import jax.numpy as jnp
from jax import lax
from jax.experimental import pallas as pl
from jax.experimental.pallas import tpu as pltpu
from jax.sharding import PartitionSpec as P


ET_OWN = 128
PT_OWN = 64
SLOTS = ET_OWN + PT_OWN
NONE = -4096
EPS = 1e-06
LANES = 128
CHUNK = 256
PIECE = 32
GROUP = 4
STARTS = (1, 1, 1, 2)
LATE = 6
F32 = jnp.float32
BF16 = jnp.bfloat16
ROOT = math.sqrt(2.0 / math.pi)


def split(value):
    high = value.astype(BF16)
    return high, (value - high.astype(F32)).astype(BF16)


def unit(table):
    return table * lax.rsqrt(jnp.sum(table * table, axis=-1, keepdims=True) + EPS)


def dot(a, b, dims=((1,), (0,))):
    return lax.dot_general(a, b, (dims, ((), ())), preferred_element_type=F32)


def place(n_enrol, n_probe):
    z, p = lax.axis_index("enrol"), lax.axis_index("probe")
    rows, chips = n_enrol // 2, n_probe // 2
    return z // rows, (z % rows) * chips + p // 2, p % 2


def twice_gelu(x):
    return x + x * jnp.tanh(x * (ROOT + (ROOT * 0.044715) * (x * x)))


def embed_kernel(n_enrol, n_probe, count_hbm, slots_hbm, images, w_first, w_second, *rest):
    chips = n_enrol * n_probe // 4
    owners = n_enrol * n_probe
    far, near = rest[:chips], rest[chips : 2 * chips]
    (img, w1, w2, x3, w3, pre, h3, v3, feature, emb, slots, table, count, ends, sem_img, sem_w1, sem_w2, sem_small) = rest[
        2 * chips :
    ]
    n_img, d_in = images.shape
    width = w_second.shape[1]
    pieces = w1.shape[0]
    block = near[0].shape[0]

    def copy_first(j):
        columns = w_first.at[:, pl.ds(pl.multiple_of(j * CHUNK, CHUNK), CHUNK)]
        return pltpu.make_async_copy(columns, w1.at[j], sem_w1.at[j])

    def copy_second(j):
        part = w_second.at[pl.ds(pl.multiple_of(j * CHUNK, CHUNK), CHUNK)]
        return pltpu.make_async_copy(part, w2.at[j], sem_w2.at[j])

    quarter = n_img // 4
    image_copies = [
        pltpu.make_async_copy(
            images.at[pl.ds(q * quarter, quarter)], img.at[pl.ds(q * quarter, quarter)], sem_img.at[q]
        )
        for q in range(4)
    ]
    for copy in image_copies:
        copy.start()
    copy_first(0).start()
    queue = [copy_first(1), copy_first(2), copy_second(0)]
    for j in range(3, pieces):
        queue += [copy_first(j), copy_second(j - 2)]
    queue += [copy_second(pieces - 2), copy_second(pieces - 1)]

    def start_more(n):
        for copy in queue[:n]:
            copy.start()
        del queue[:n]

    small = [
        pltpu.make_async_copy(count_hbm, count, sem_small.at[0]),
        pltpu.make_async_copy(slots_hbm, slots, sem_small.at[1]),
    ]
    for copy in small:
        copy.start()

    def thrice(source, target, rows):
        for r in range(0, rows, PIECE):
            high, low = split(source[pl.ds(r, PIECE), :])
            target[pl.ds(r, PIECE), :] = high
            target[pl.ds(rows + r, PIECE), :] = high
            target[pl.ds(2 * rows + r, PIECE), :] = low

    def first(s):
        pre[s] = dot(x3[...], w3[s])

    def load(j, s):
        thrice(w1.at[j], w3.at[s], d_in)

    def bend(s):
        for r in range(0, n_img, PIECE):
            at = pl.ds(r, PIECE)
            high, low = split(twice_gelu(pre[s, at, :]))
            h3[s, at, 0:CHUNK] = high
            h3[s, at, CHUNK : 2 * CHUNK] = low
            h3[s, at, 2 * CHUNK :] = high

    def second(j, s):
        thrice(w2.at[j], v3.at[s], CHUNK)
        feature[...] = feature[...] + dot(h3[s], v3[s])

    for q, copy in enumerate(image_copies):
        copy.wait()
        start_more(STARTS[q])
        for r in range(q * quarter, (q + 1) * quarter, PIECE):
            at = pl.ds(r, PIECE)
            high, low = split(img[at, :])
            x3[at, 0:d_in] = high
            x3[at, d_in : 2 * d_in] = low
            x3[at, 2 * d_in :] = high
    copy_first(0).wait()
    start_more(len(queue) - LATE)
    load(0, 0)
    first(0)
    copy_first(1).wait()
    start_more(len(queue))
    load(1, 1)
    feature[...] = jnp.zeros_like(feature)

    def trip(i, carry):
        @pl.when(i == 0)
        def _():
            for j in range(GROUP):
                copy_first(j + 2).wait()
                copy_second(j).wait()

        @pl.when(i == 1)
        def _():
            for j in range(GROUP, pieces):
                if j + 2 < pieces:
                    copy_first(j + 2).wait()
                copy_second(j).wait()

        for step in range(GROUP):
            j, s = GROUP * i + step, step % 2
            bend(s)
            first(1 - s)
            load(jnp.minimum(j + 2, pieces - 1), s)
            second(j, s)
        return carry

    lax.fori_loop(0, pieces // GROUP, trip, 0)

    for copy in small:
        copy.wait()
    ends[0] = 0
    rows = slots.shape[0]
    position = lax.broadcasted_iota(jnp.int32, (rows, LANES), 0) * LANES
    position = position + lax.broadcasted_iota(jnp.int32, (rows, LANES), 1)
    odd = jnp.zeros((rows, LANES), jnp.int32)
    total = jnp.int32(0)
    for o in range(owners):
        total = total + count[0, o]
        ends[o + 1] = total
        odd = jnp.where(position >= total, (o + 1) % 2, odd)
    table[...] = jnp.full(table.shape, NONE, jnp.int32)
    table[0:rows, :] = slots[...] + SLOTS * odd

    tiles = width // LANES
    for r in range(0, n_img, PIECE):
        rows = unit(0.5 * feature[pl.ds(r, PIECE), :])
        for t in range(tiles):
            emb[t, pl.ds(r, PIECE), :] = rows[:, t * LANES : (t + 1) * LANES]
    for t in range(tiles):
        emb[t, n_img : n_img + block, :] = jnp.zeros((block, LANES), F32)

    half, chip, _ = place(n_enrol, n_probe)
    lane = lax.broadcasted_iota(jnp.int32, (1, LANES), 1)

    def window(start, size):
        row, shift = start // LANES, start % LANES
        back = (LANES - shift) % LANES
        one = pltpu.roll(table[pl.ds(row, 1), :], back, 1)
        two = pltpu.roll(table[pl.ds(row + 1, 1), :], back, 1)
        ids = jnp.where(lane < LANES - shift, one, two)
        return jnp.where(lane < size, ids, NONE).astype(F32)

    for k in range(chips):
        to = chip ^ k
        for side in range(2):
            pair = (half if side else 1 - half) * chips + to
            start, stop = ends[2 * pair], ends[2 * pair + 2]
            out = near[k] if side else far[k]
            for t in range(tiles):
                out[0:block, t * LANES : (t + 1) * LANES] = emb[t, pl.ds(start, block), :]
            far[k][block + side : block + side + 1, 0:LANES] = window(start, stop - start)


def embed(n_enrol, n_probe, images, w_first, w_second, slots, count):
    chips = n_enrol * n_probe // 4
    n_img, d_in = images.shape
    width = w_second.shape[1]
    pieces = w_second.shape[0] // CHUNK
    block = 4 * n_img // (n_enrol * n_probe)
    vmem = pl.BlockSpec(memory_space=pltpu.VMEM)
    hbm = pl.BlockSpec(memory_space=pltpu.HBM)
    inputs = count, slots.reshape(n_img // LANES, LANES), images, w_first, w_second
    outs = pl.pallas_call(
        functools.partial(embed_kernel, n_enrol, n_probe),
        out_shape=[jax.ShapeDtypeStruct((block + 8, width), F32)] * chips
        + [jax.ShapeDtypeStruct((block, width), F32)] * chips,
        in_specs=[hbm] * 5,
        out_specs=[vmem] * (2 * chips),
        scratch_shapes=[
            pltpu.VMEM((n_img, d_in), F32),
            pltpu.VMEM((pieces, d_in, CHUNK), F32),
            pltpu.VMEM((pieces, CHUNK, width), F32),
            pltpu.VMEM((n_img, 3 * d_in), BF16),
            pltpu.VMEM((2, 3 * d_in, CHUNK), BF16),
            pltpu.VMEM((2, n_img, CHUNK), F32),
            pltpu.VMEM((2, n_img, 3 * CHUNK), BF16),
            pltpu.VMEM((2, 3 * CHUNK, width), BF16),
            pltpu.VMEM((n_img, width), F32),
            pltpu.VMEM((width // LANES, n_img + block, LANES), F32),
            pltpu.VMEM((n_img // LANES, LANES), jnp.int32),
            pltpu.VMEM((n_img // LANES + 8 - n_img // LANES % 8, LANES), jnp.int32),
            pltpu.SMEM((1, n_enrol * n_probe), jnp.int32),
            pltpu.SMEM((n_enrol * n_probe + 1,), jnp.int32),
            pltpu.SemaphoreType.DMA((4,)),
            pltpu.SemaphoreType.DMA((pieces,)),
            pltpu.SemaphoreType.DMA((pieces,)),
            pltpu.SemaphoreType.DMA((2,)),
        ],
        compiler_params=pltpu.CompilerParams(vmem_limit_bytes=52 << 20),
        name="embed",
    )(*[pltpu.with_memory_space_constraint(x, pltpu.HBM) for x in inputs])
    return outs[:chips], outs[chips:]


def picked(half, ids, side, rows):
    block = rows.shape[0] if side else rows.shape[0] - 8
    at = ids.shape[0] - 8 + side
    want = ids[at : at + 1, 0:LANES][:, :block].astype(jnp.int32)
    core = lax.axis_index("probe") % 2
    want = want - (core ^ half) * SLOTS
    slot = lax.broadcasted_iota(jnp.int32, (SLOTS, block), 0)
    pick = (slot == want).astype(F32).astype(BF16)
    high, low = split(rows[0:block, :])
    return dot(pick, high) + dot(pick, low)


def pool_own_kernel(side, ids, rows, mine, other):
    mine[...] = picked(0, ids, side, rows)
    other[...] = picked(1, ids, side, rows)


def pool_one_kernel(half, ids, rows, out):
    out[...] = picked(half, ids, 1, rows)


def pool_kernel(side, half, count, *refs):
    ids, rows = refs[:count], refs[count : 2 * count] if side else refs[:count]
    before, out = refs[-2:]
    sums = before[...]
    for k in range(count):
        sums = sums + picked(half, ids[k], side, rows[k])
    out[...] = sums


def local(kernel, outs, *args, limit=8 << 20, kind=F32):
    vmem = pl.BlockSpec(memory_space=pltpu.VMEM)
    return pl.pallas_call(
        kernel,
        out_shape=[jax.ShapeDtypeStruct(shape, kind) for shape in outs],
        in_specs=[vmem] * len(args),
        out_specs=[vmem] * len(outs),
        compiler_params=pltpu.CompilerParams(vmem_limit_bytes=limit),
    )(*args)


def add_kernel(a, b, out):
    out[...] = a[...] + b[...]


def prepare_kernel(own, other, own_out, other_out):
    width = own.shape[1]
    for table, out in ((own, own_out), (other, other_out)):
        out[:, :width], out[:, width:] = split(unit(table[...]))


def score_kernel(n_enrol, n_probe, scale, bias, *refs):
    rows, cols = n_enrol // 2, n_probe // 2
    enrol, probe = refs[: 2 * cols], refs[2 * cols : 2 * cols + 2 * rows]
    out, e3, p3 = refs[2 * cols + 2 * rows :]
    width = probe[0].shape[1]
    z, p = lax.axis_index("enrol"), lax.axis_index("probe")

    def put(table, start, size, high_low):
        at = pl.ds(pl.multiple_of(start * size, size), size)
        for t, part in enumerate(high_low):
            table[at, t * width : (t + 1) * width] = part

    for k in range(rows):
        for side in range(2):
            high, low = split(unit(probe[2 * k + side][...]))
            put(p3, z ^ k ^ (side * rows), PT_OWN, (high, high, low))
    for k in range(n_probe):
        if k < 2:
            high, low = enrol[k][:, :width], enrol[k][:, width:]
        else:
            high, low = split(unit(enrol[k][...]))
        put(e3, p ^ k, ET_OWN, (high, low, high))
    for start in range(0, e3.shape[0], 2 * ET_OWN):
        at = pl.ds(start, 2 * ET_OWN)
        cosine = dot(e3[at, :], p3[...], ((1,), (1,)))
        out[at, :] = jax.nn.sigmoid(scale[0] * cosine + bias[0]).astype(BF16)


def score(n_enrol, n_probe, scale, bias, enrol, probe):
    width = probe[0].shape[1]
    vmem = pl.BlockSpec(memory_space=pltpu.VMEM)
    smem = pl.BlockSpec(memory_space=pltpu.SMEM)
    return pl.pallas_call(
        functools.partial(score_kernel, n_enrol, n_probe),
        out_shape=jax.ShapeDtypeStruct((n_probe * ET_OWN, n_enrol * PT_OWN), BF16),
        in_specs=[smem, smem] + [vmem] * (len(enrol) + len(probe)),
        out_specs=vmem,
        scratch_shapes=[
            pltpu.VMEM((n_probe * ET_OWN, 3 * width), BF16),
            pltpu.VMEM((n_enrol * PT_OWN, 3 * width), BF16),
        ],
        compiler_params=pltpu.CompilerParams(vmem_limit_bytes=8 << 20),
        name="score",
    )(scale, bias, *enrol, *probe)


def solution(mesh):
    n_enrol, n_probe = mesh.shape["enrol"], mesh.shape["probe"]
    rows, cols = n_enrol // 2, n_probe // 2
    chips = rows * cols

    def flip(value, enrol_bits, probe_bits):
        pairs = [
            (z * n_probe + p, (z ^ enrol_bits) * n_probe + (p ^ probe_bits))
            for z in range(n_enrol)
            for p in range(n_probe)
        ]
        return lax.ppermute(value, ("enrol", "probe"), pairs)

    def across_chips(blocks):
        moved = []
        for k in range(1, chips):
            moved.append(flip(blocks[k], k // cols, 2 * (k % cols)))
        return moved

    def body(images, w_first, w_second, scale, bias, template_slot, media_counts):
        far, near = embed(n_enrol, n_probe, images, w_first, w_second, template_slot, media_counts)
        sums = (SLOTS, w_second.shape[1])
        far_in = across_chips(far)
        near_in = across_chips(near)
        kernel = functools.partial(pool_own_kernel, 0)
        far_mine, far_other = local(kernel, [sums] * 2, far[0], far[0])
        kernel = functools.partial(pool_one_kernel, 0)
        (near_mine,) = local(kernel, [sums], far[0], near[0])
        kernel = functools.partial(pool_one_kernel, 1)
        (near_other,) = local(kernel, [sums], far[0], near[0])

        def pool(side, half, *args):
            kernel = functools.partial(pool_kernel, side, half, chips - 1)
            return local(kernel, [sums], *args)[0]

        far_other = pool(0, 1, *far_in, far_other)
        far_other = flip(far_other, 0, 1)
        far_mine = pool(0, 0, *far_in, far_mine)
        far_enrol, far_probe = lax.optimization_barrier(
            (far_mine[:ET_OWN] + far_other[:ET_OWN], far_mine[ET_OWN:] + far_other[ET_OWN:])
        )
        enrol_far = flip(far_enrol, rows, 0)
        own_far = flip(far_probe, rows, 0)
        near_other = pool(1, 1, *far_in, *near_in, near_other)
        near_mine = pool(1, 0, *far_in, *near_in, near_mine)
        near_other = flip(near_other, 0, 1)
        near_probe = near_mine[ET_OWN:] + near_other[ET_OWN:]
        probe_far = flip(near_probe, rows, 0)
        (near_sum,) = local(add_kernel, [sums], near_mine, near_other)
        enrol = near_sum[:ET_OWN] + enrol_far
        own_probe = near_sum[ET_OWN:] + own_far
        across_probe = far_probe + probe_far
        probe_parts = []
        for k in range(rows):
            for part in (own_probe, across_probe):
                probe_parts.append(flip(part, k, 0) if k else part)
        pair = (ET_OWN, 2 * enrol.shape[1])
        enrol_parts = [enrol, flip(enrol, 0, 1)]
        enrol_parts = [*local(prepare_kernel, [pair] * 2, *enrol_parts, kind=BF16)]
        for k in range(1, cols):
            part = flip(enrol, 0, 2 * k)
            enrol_parts += [part, flip(part, 0, 1)]
        return score(n_enrol, n_probe, scale, bias, enrol_parts, probe_parts)

    return jax.shard_map(
        body,
        mesh=mesh,
        in_specs=(
            P(("groups", "enrol", "probe"), None),
            P(),
            P(),
            P(),
            P(),
            P(("groups", "enrol", "probe")),
            P(("groups", "enrol", "probe"), None),
        ),
        out_specs=P(("groups", "enrol"), "probe"),
        check_vma=False,
    )
```
